32 devices in a mesh: groups: 2 (over x), blk: 4 (over y, core), rows: 4 (over z).
Axes of the slice: x: 2, y: 2, z: 4, core: 2. Of those that a mesh axis runs over, the one named last changes fastest.
Arguments:
- frame_one: float32 [4096, 256], P(('groups', 'blk', 'rows')), parts along dimension 0, may hold values from -6 to 6
- frame_two: float32 [4096, 256], P(('groups', 'blk', 'rows')), parts along dimension 0, may hold values from -6 to 6
- cot_zero: float32 [4096, 2048], P(('groups', 'blk', 'rows')), parts along dimension 0, may hold values from -0.375 to 0.375
- cot_one: float32 [4096, 512], P(('groups', 'blk', 'rows')), parts along dimension 0, may hold values from -1.5 to 1.5
- cot_two: float32 [4096, 128], P(('groups', 'blk', 'rows')), parts along dimension 0, may hold values from -6 to 6
- cot_three: float32 [4096, 32], P(('groups', 'blk', 'rows')), parts along dimension 0, may hold values from -24 to 24
Outputs:
- corr_zero: float32 [4096, 2048], P(('groups', 'blk', 'rows')), parts along dimension 0
- corr_one: float32 [4096, 512], P(('groups', 'blk', 'rows')), parts along dimension 0
- corr_two: float32 [4096, 128], P(('groups', 'blk', 'rows')), parts along dimension 0
- corr_three: float32 [4096, 32], P(('groups', 'blk', 'rows')), parts along dimension 0
- grad_one: float32 [256, 4096], P('rows', ('groups', 'blk')), parts along dimension 1
- grad_two: float32 [256, 4096], P('rows', ('groups', 'blk')), parts along dimension 1
The draws below stay inside these ranges and needn't reach their ends.
There are 2 independent parts, one for each index of `groups`. The reference program is written for one: setup_inputs(seed, part) draws one part's arguments, and reference() takes and returns one part's arrays. A program takes and returns all parts, laid end to end along the dimension named above; each array names one. Nothing has to cross between parts.
All inputs are finite; a program needn't handle non-finite values.
Results may differ from the reference program's by a relative error of at most 0.0001.
Values sent between devices are 32-bit elements; how exact they have to be, the bound alone decides.
A program may use at most 64 MiB of HBM per device.

```python
import math
import jax
import jax.numpy as jnp
from jax import lax

C = 256
LEVELS = 4
TROWS = 8
W2 = 64
BAND = 128
P2 = 2048
P1 = 2048
N_BLK = 4
N_ROWS = 4


def levels(own_key, shape, pieces, least, high):
    factor_of = 1.0
    for position, parts in pieces:
        draws = jax.random.uniform(jax.random.fold_in(jax.random.fold_in(own_key, 6), position), (parts,), jnp.float32, least / len(pieces), high / len(pieces))
        factor_of = factor_of * jnp.repeat(jnp.exp(draws), shape[position] // parts).reshape((-1,) + (1,) * (len(shape) - 1 - position))
    return factor_of


def normal_values(key, extent, width, most, shards=(), held_as=jnp.bfloat16):
    loudness = levels(key, extent, shards, -0.22, 0.18) if shards else 1.0
    values = jax.random.normal(key, extent, jnp.float32) * width * loudness
    return jnp.minimum(jnp.maximum(values, -most), most).astype(held_as)


def setup_inputs(seed: int = 0, part: int = 0) -> dict:
    splits = jax.random.split(jax.random.key(seed), 7)
    own_keys = jax.random.split(jax.random.fold_in(splits[6], part), 7)
    return {
        "frame_one": normal_values(own_keys[0], (P1, C), 1.0, 6.0, ((0, 16),), jnp.float32),
        "frame_two": normal_values(own_keys[1], (P2, C), 1.0, 6.0, ((0, 16),), jnp.float32),
        "cot_zero": normal_values(own_keys[2], (P1, P2), 0.0625, 0.375, ((0, 16),), jnp.float32),
        "cot_one": normal_values(own_keys[3], (P1, P2 // 4), 0.25, 1.5, ((0, 16),), jnp.float32),
        "cot_two": normal_values(own_keys[4], (P1, P2 // 16), 1.0, 6.0, ((0, 16),), jnp.float32),
        "cot_three": normal_values(own_keys[5], (P1, P2 // 64), 4.0, 24.0, ((0, 16),), jnp.float32),
    }


highest = lax.Precision.HIGHEST

def pool_once(volume, rows_now, cols_now):
    count_rows = volume.shape[0]
    shaped = volume.reshape(count_rows, rows_now // 2, 2, cols_now // 2, 2)
    return lax.optimization_barrier(jnp.mean(shaped, axis=(2, 4))).reshape(count_rows, rows_now // 2 * (cols_now // 2))

def spread_up(coarse, rows_now, cols_now):
    count_rows = coarse.shape[0]
    shaped = coarse.reshape(count_rows, rows_now, 1, cols_now, 1)
    widened = jnp.broadcast_to(shaped, (count_rows, rows_now, 2, cols_now, 2))
    return widened.reshape(count_rows, 4 * rows_now * cols_now) * 0.25

def reference(frame_one, frame_two, cot_zero, cot_one, cot_two, cot_three):
    inv_root = 1.0 / math.sqrt(C)
    image_rows = TROWS * N_BLK
    block_rows = BAND * N_ROWS
    cots = (cot_zero, cot_one, cot_two, cot_three)
    shaped_one = frame_one.reshape(N_BLK, block_rows, C)
    shaped_cots = tuple((cot.reshape(N_BLK, block_rows, cot.shape[1]) for cot in cots))

    def block_step(grad_accum, inputs):
        rows_blk = inputs[0]
        block_cots = inputs[1:]
        volume = jnp.dot(rows_blk, frame_two.T, precision=highest, preferred_element_type=jnp.float32) * inv_root
        levels_out = [volume]
        rows_now = image_rows
        cols_now = W2
        for level_idx in range(LEVELS - 1):
            volume = pool_once(volume, rows_now, cols_now)
            rows_now = rows_now // 2
            cols_now = cols_now // 2
            levels_out.append(volume)
        cot_total = block_cots[LEVELS - 1]
        for level_idx in range(LEVELS - 2, -1, -1):
            cot_total = block_cots[level_idx] + spread_up(cot_total, rows_now, cols_now)
            rows_now = rows_now * 2
            cols_now = cols_now * 2
        scaled = cot_total * inv_root
        grad_rows = jnp.dot(scaled, frame_two, precision=highest, preferred_element_type=jnp.float32)
        grad_accum = grad_accum + jnp.dot(scaled.T, rows_blk, precision=highest, preferred_element_type=jnp.float32)
        return (grad_accum, tuple(levels_out) + (grad_rows,))
    start_accum = jnp.zeros((P2, C), jnp.float32)
    grad_accum, outputs = lax.scan(block_step, start_accum, (shaped_one,) + shaped_cots)
    corr_zero = outputs[0].reshape(P1, P2)
    corr_one = outputs[1].reshape(P1, P2 // 4)
    corr_two = outputs[2].reshape(P1, P2 // 16)
    corr_three = outputs[3].reshape(P1, P2 // 64)
    grad_one = outputs[4].reshape(P1, C).T
    grad_two = grad_accum.T
    return (corr_zero, corr_one, corr_two, corr_three, grad_one, grad_two)
```

```python
import functools
import math

import jax
import jax.numpy as jnp
from jax import lax
from jax.experimental import pallas as pl
from jax.experimental.pallas import tpu as pltpu
from jax.sharding import PartitionSpec as P

TROWS = 8
W2 = 64
CORES = 2
TILE = TROWS * W2
POOL1 = TILE // 4
POOL2 = TILE // 16
POOL3 = TILE // 64
POOLED = 2 * POOL1

f32 = jnp.float32
bf16 = jnp.bfloat16


def split(x):
    high = x.astype(bf16)
    low = (x - high.astype(f32)).astype(bf16)
    return high, low


def mm(a, b, ca, cb):
    return lax.dot_general(a, b, (((ca,), (cb,)), ((), ())), preferred_element_type=f32)


def pool_table():
    shape = (TILE, POOLED)
    pixel = lax.broadcasted_iota(jnp.int32, shape, 0)
    slot = lax.broadcasted_iota(jnp.int32, shape, 1)
    row, col = pixel // W2, pixel % W2
    one = (row // 2) * (W2 // 2) + col // 2
    two = (row // 4) * (W2 // 4) + col // 4 + POOL1
    three = (row // 8) * (W2 // 8) + col // 8 + POOL1 + POOL2
    value = jnp.where(slot == one, 0.25, 0.0)
    value = jnp.where(slot == two, 0.0625, value)
    value = jnp.where(slot == three, 0.015625, value)
    return value.astype(bf16)


def kernel(tiles, rows_n, f1_in, f2_in, c0_in, c1_in, c2_in, c3_in,
           o0, o1, o2, o3, g1_out, g2_out,
           f1, f2, c0, c1, c2, c3, coarse, scaled, table, f1s, f1t, acc, cin, yin, zin,
           corr, pooled, b2, b3, gacc, g1t,
           in_sem, out_sem, ag_recv, zs_sem, ys_sem, cs_sem,
           rc_send, rc_recv, ry_send, ry_recv, rz_send, rz_recv, g_send, g_recv):
    band = f1.shape[0]
    chans = f1.shape[1]
    band2 = f2_in.shape[0]
    ys_n = tiles // CORES
    inv_root = 1.0 / math.sqrt(chans)
    blk = lax.axis_index("blk")
    z = lax.axis_index("rows")
    core = blk % CORES
    y = blk // CORES
    other = 1 - core
    sib = {"blk": y * CORES + other}

    def at_z(k):
        return (z + k) % rows_n

    def at_y(k):
        return (y + k) % ys_n

    def span(t, zz):
        return pl.ds(pl.multiple_of(t * TILE + zz * band2, 8), band2)

    loads = {}
    for i, (name, src, dst) in enumerate((
            ("f1", f1_in, f1), ("c3", c3_in, c3), ("c2", c2_in, c2), ("c1", c1_in, c1),
            ("c0", c0_in, c0), ("f2", f2_in, f2.at[span(blk, z), :]))):
        loads[name] = pltpu.make_async_copy(src, dst, in_sem.at[i])
        loads[name].start()

    peers = [{"rows": at_z(k)} for k in range(1, rows_n)]
    peers += [{"blk": at_y(k) * CORES + core} for k in range(1, ys_n)]
    peers += [sib]
    barrier = pltpu.get_barrier_semaphore()
    for peer in peers:
        pl.semaphore_signal(barrier, inc=1, device_id=peer)
    table[...] = pool_table()
    pl.semaphore_wait(barrier, len(peers))

    sent = []

    def send(src, dst, ssem, rsem, peer):
        copy = pltpu.make_async_remote_copy(
            src_ref=src, dst_ref=dst, send_sem=ssem, recv_sem=rsem,
            device_id=peer, device_id_type=pl.DeviceIdType.MESH)
        copy.start()
        sent.append(copy)

    def await_(ref, rsem):
        pltpu.make_async_copy(ref, ref, rsem).wait()

    def ag_wait(t, zz):
        await_(f2.at[span(t, zz), :], ag_recv.at[t * rows_n + zz])

    def to_sib(t, zz, src=None):
        where = f2.at[span(t, zz), :]
        i = t * rows_n + zz
        send(where if src is None else src, where, cs_sem.at[i], ag_recv.at[i], sib)

    def to_y(k, zz, src=None):
        where = f2.at[span(blk, zz), :]
        send(where if src is None else src, where, ys_sem.at[k - 1, zz],
             ag_recv.at[blk * rows_n + zz], {"blk": at_y(k) * CORES + core})

    order = sorted(range(1, rows_n), key=lambda k: -min(k, rows_n - k))
    own = f2.at[span(blk, z), :]
    for k in order:
        send(f2_in, own, zs_sem.at[k - 1], ag_recv.at[blk * rows_n + z], {"rows": at_z(k)})
    for k in range(1, ys_n):
        to_y(k, z, f2_in)
    to_sib(blk, z, f2_in)

    loads["f1"].wait()
    high, low = split(f1[...])
    f1s[0:band, :] = high
    f1s[band:, :] = low
    turned = f1[...].T
    high, low = split(turned)
    f1t[:, 0:band] = high
    f1t[:, band:] = low
    loads["c3"].wait()
    loads["c2"].wait()
    loads["c1"].wait()
    for t in range(tiles):
        coarse[t] = jnp.concatenate(
            [c1[:, t * POOL1:(t + 1) * POOL1], c2[:, t * POOL2:(t + 1) * POOL2],
             c3[:, t * POOL3:(t + 1) * POOL3],
             jnp.zeros((band, POOLED - POOL1 - POOL2 - POOL3), f32)], axis=1)
    loads["c0"].wait()

    def band_sum(t):
        high, low = split(coarse[t])
        spread = mm(jnp.concatenate([high, low], axis=0), table[...], 1, 1)
        total = c0[:, pl.ds(pl.multiple_of(t * TILE, TILE), TILE)] + (spread[:band] + spread[band:])
        high, low = split(total * inv_root)
        scaled[t, 0:band, :] = high
        scaled[t, band:, :] = low
        twice = jnp.concatenate([high, high], axis=0)
        value = mm(f1t[...], twice, 1, 0) + mm(f1t[:, 0:band], low, 1, 0)
        acc[t] = value.reshape(rows_n, chans // rows_n, TILE)

    for k in list(range(1, ys_n)) + [0]:
        yy = at_y(k)
        band_sum(yy * CORES + other)
        send(acc.at[yy * CORES + other], cin.at[yy], rc_send.at[yy], rc_recv.at[yy], sib)
        band_sum(yy * CORES + core)

    def chip_sum(yy):
        await_(cin.at[yy], rc_recv.at[yy])
        t = yy * CORES + core
        acc[t] += cin[yy]

    for k in range(1, ys_n):
        yy = at_y(k)
        chip_sum(yy)
        for j in order + [0]:
            zz = at_z(j)
            send(acc.at[yy * CORES + core, zz], yin.at[k - 1, zz], ry_send.at[k - 1, zz],
                 ry_recv.at[k - 1, zz], {"blk": yy * CORES + core})

    for k in reversed(order):
        zz = at_z(k)
        ag_wait(blk, zz)
        for j in range(1, ys_n):
            to_y(j, zz)
        to_sib(blk, zz)
    chip_sum(y)
    loads["f2"].wait()

    outs = []

    def emit(src, dst, sem):
        copy = pltpu.make_async_copy(src, dst, sem)
        copy.start()
        outs.append(copy)

    def tile_work(i, t):
        block = f2[pl.ds(pl.multiple_of(t * TILE, TILE), TILE), :]
        high, low = split(block)
        both = mm(f1s[...], high, 1, 1)
        value = (both[:band] + both[band:] + mm(f1s[0:band, :], low, 1, 1)) * inv_root
        corr[t] = value
        emit(corr.at[t], o0.at[:, pl.ds(pl.multiple_of(t * TILE, TILE), TILE)], out_sem.at[0, i])
        vh, vl = split(value)
        both = mm(jnp.concatenate([vh, vl], axis=0), table[...], 1, 0)
        pooled[t] = both[:band] + both[band:]
        emit(pooled.at[t, :, 0:POOL1], o1.at[:, pl.ds(pl.multiple_of(t * POOL1, POOL1), POOL1)],
             out_sem.at[1, i])
        both = mm(scaled[t], high, 1, 0)
        grad = both[:band] + both[band:] + mm(scaled[t, 0:band, :], low, 1, 0)
        if i == 0:
            gacc[...] = grad
        else:
            gacc[...] += grad

    tile_work(0, blk)

    for j in order + [0]:
        zz = at_z(j)
        for k in range(1, ys_n):
            await_(yin.at[k - 1, zz], ry_recv.at[k - 1, zz])
            acc[blk, zz] += yin[k - 1, zz]
        if j:
            send(acc.at[blk, zz], zin.at[j - 1], rz_send.at[j - 1], rz_recv.at[j - 1], {"rows": zz})

    for zz in range(rows_n):
        ag_wait(y * CORES + other, zz)
    tile_work(1, y * CORES + other)

    done = 2
    for k in range(1, ys_n):
        t = at_y(k) * CORES + core
        for j in [0] + list(reversed(order)):
            zz = at_z(j)
            ag_wait(t, zz)
            to_sib(t, zz)
        tile_work(done, t)
        done += 1
    for k in range(1, ys_n):
        t = at_y(k) * CORES + other
        for zz in range(rows_n):
            ag_wait(t, zz)
        tile_work(done, t)
        done += 1

    g1t[...] = gacc[...].T.reshape(rows_n, chans // rows_n, band)
    mine = pl.ds(pl.multiple_of(z * band, band), band)
    for k in order:
        zz = at_z(k)
        send(g1t.at[zz], g1_out.at[:, mine], g_send.at[k - 1], g_recv.at[k - 1], {"rows": zz})
    g1_out[:, mine] = g1t[z]
    b2[...] = jnp.concatenate([pooled[t, :, POOL1:POOL1 + POOL2] for t in range(tiles)], axis=1)
    emit(b2, o2, out_sem.at[2, 0])
    b3[...] = jnp.concatenate(
        [pooled[t, :, POOL1 + POOL2:POOL1 + POOL2 + POOL3] for t in range(tiles)], axis=1)
    emit(b3, o3, out_sem.at[2, 1])
    total = acc[blk, z]
    for k in range(1, rows_n):
        await_(zin.at[k - 1], rz_recv.at[k - 1])
        total += zin[k - 1]
    g2_out[...] = total
    for k in range(1, rows_n):
        zz = (z + rows_n - k) % rows_n
        await_(g1_out.at[:, pl.ds(pl.multiple_of(zz * band, band), band)], g_recv.at[k - 1])
    for copy in outs:
        copy.wait()
    for copy in sent:
        copy.wait_send()


def on_device(tiles, rows_n, frame_one, frame_two, cot_zero, cot_one, cot_two, cot_three):
    band, chans = frame_one.shape
    ys_n = tiles // CORES
    part = chans // rows_n
    cots = (cot_zero, cot_one, cot_two, cot_three)
    hbm = pl.BlockSpec(memory_space=pl.ANY)
    vmem = pl.BlockSpec(memory_space=pltpu.VMEM)
    dma = pltpu.SemaphoreType.DMA
    return pl.pallas_call(
        functools.partial(kernel, tiles, rows_n),
        out_shape=tuple(jax.ShapeDtypeStruct(cot.shape, f32) for cot in cots) + (
            jax.ShapeDtypeStruct((part, band * rows_n), f32),
            jax.ShapeDtypeStruct((part, TILE), f32)),
        in_specs=[hbm] * 6,
        out_specs=(hbm,) * 4 + (vmem,) * 2,
        scratch_shapes=[
            pltpu.VMEM((band, chans), f32),
            pltpu.VMEM((tiles * TILE, chans), f32),
            pltpu.VMEM(cot_zero.shape, f32),
            pltpu.VMEM(cot_one.shape, f32),
            pltpu.VMEM(cot_two.shape, f32),
            pltpu.VMEM(cot_three.shape, f32),
            pltpu.VMEM((tiles, band, POOLED), f32),
            pltpu.VMEM((tiles, 2 * band, TILE), bf16),
            pltpu.VMEM((TILE, POOLED), bf16),
            pltpu.VMEM((2 * band, chans), bf16),
            pltpu.VMEM((chans, 2 * band), bf16),
            pltpu.VMEM((tiles, rows_n, part, TILE), f32),
            pltpu.VMEM((ys_n, rows_n, part, TILE), f32),
            pltpu.VMEM((ys_n - 1, rows_n, part, TILE), f32),
            pltpu.VMEM((rows_n - 1, part, TILE), f32),
            pltpu.VMEM((tiles, band, TILE), f32),
            pltpu.VMEM((tiles, band, POOLED), f32),
            pltpu.VMEM(cot_two.shape, f32),
            pltpu.VMEM(cot_three.shape, f32),
            pltpu.VMEM((band, chans), f32),
            pltpu.VMEM((rows_n, part, band), f32),
            dma((6,)),
            dma((3, max(tiles, 2))),
            dma((tiles * rows_n,)),
            dma((rows_n - 1,)),
            dma((ys_n - 1, rows_n)),
            dma((tiles * rows_n,)),
            dma((ys_n,)), dma((ys_n,)),
            dma((ys_n - 1, rows_n)), dma((ys_n - 1, rows_n)),
            dma((rows_n - 1,)), dma((rows_n - 1,)),
            dma((rows_n - 1,)), dma((rows_n - 1,)),
        ],
        compiler_params=pltpu.CompilerParams(
            collective_id=0, has_side_effects=True, vmem_limit_bytes=58 << 20),
    )(frame_one, frame_two, *cots)


def solution(mesh):
    band = P(("groups", "blk", "rows"), None)
    turned = P("rows", ("groups", "blk"))
    return jax.shard_map(
        functools.partial(on_device, mesh.shape["blk"], mesh.shape["rows"]),
        mesh=mesh,
        in_specs=(band,) * 6,
        out_specs=(band,) * 4 + (turned,) * 2,
        check_vma=False,
    )
```

```python
import functools
import math

import jax
import jax.numpy as jnp
from jax import lax
from jax.experimental import pallas as pl
from jax.experimental.pallas import tpu as pltpu
from jax.sharding import PartitionSpec as P

TROWS = 8
W2 = 64
CORES = 2
TILE = TROWS * W2
POOL1 = TILE // 4
POOL2 = TILE // 16
POOL3 = TILE // 64
POOLED = 2 * POOL1

f32 = jnp.float32
bf16 = jnp.bfloat16


def split(x):
    high = x.astype(bf16)
    low = (x - high.astype(f32)).astype(bf16)
    return high, low


def mm(a, b, ca, cb):
    return lax.dot_general(a, b, (((ca,), (cb,)), ((), ())), preferred_element_type=f32)


def pool_table():
    shape = (TILE, POOLED)
    pixel = lax.broadcasted_iota(jnp.int32, shape, 0)
    slot = lax.broadcasted_iota(jnp.int32, shape, 1)
    row, col = pixel // W2, pixel % W2
    one = (row // 2) * (W2 // 2) + col // 2
    two = (row // 4) * (W2 // 4) + col // 4 + POOL1
    three = (row // 8) * (W2 // 8) + col // 8 + POOL1 + POOL2
    value = jnp.where(slot == one, 0.25, 0.0)
    value = jnp.where(slot == two, 0.0625, value)
    value = jnp.where(slot == three, 0.015625, value)
    return value.astype(bf16)


def kernel(tiles, rows_n, f1_in, f2_in, c0_in, c1_in, c2_in, c3_in,
           o0, o1, o2, o3, g1_out, g2_out,
           f1, f2, c0, c1, c2, c3t, coarse, scaled, table, f1s, f1t, acc, cin, yin, zin,
           pooled, gacc, g1t,
           in_sem, ag_recv, zs_sem, ys_sem, cs_sem,
           rc_send, rc_recv, ry_send, ry_recv, rz_send, rz_recv, g_send, g_recv):
    band = f1.shape[0]
    chans = f1.shape[1]
    band2 = f2_in.shape[0]
    ys_n = tiles // CORES
    inv_root = 1.0 / math.sqrt(chans)
    blk = lax.axis_index("blk")
    z = lax.axis_index("rows")
    core = blk % CORES
    y = blk // CORES
    other = 1 - core
    sib = {"blk": y * CORES + other}

    def at_z(k):
        return (z + k) % rows_n

    def at_y(k):
        return (y + k) % ys_n

    def span(t, zz):
        return pl.ds(pl.multiple_of(t * TILE + zz * band2, 8), band2)

    loads = {}
    for i, (name, src, dst) in enumerate((
            ("f1", f1_in, f1), ("c3", c3_in, c3t), ("c2", c2_in, c2), ("c1", c1_in, c1),
            ("c0", c0_in, c0), ("f2", f2_in, f2.at[span(blk, z), :]))):
        loads[name] = pltpu.make_async_copy(src, dst, in_sem.at[i])
        loads[name].start()

    peers = [{"rows": at_z(k)} for k in range(1, rows_n)]
    peers += [{"blk": at_y(k) * CORES + core} for k in range(1, ys_n)]
    peers += [sib]
    barrier = pltpu.get_barrier_semaphore()
    for peer in peers:
        pl.semaphore_signal(barrier, inc=1, device_id=peer)
    table[...] = pool_table()
    pl.semaphore_wait(barrier, len(peers))

    sent = []

    def send(src, dst, ssem, rsem, peer):
        copy = pltpu.make_async_remote_copy(
            src_ref=src, dst_ref=dst, send_sem=ssem, recv_sem=rsem,
            device_id=peer, device_id_type=pl.DeviceIdType.MESH)
        copy.start()
        sent.append(copy)

    def await_(ref, rsem):
        pltpu.make_async_copy(ref, ref, rsem).wait()

    def ag_wait(t, zz):
        await_(f2.at[span(t, zz), :], ag_recv.at[t * rows_n + zz])

    def to_sib(t, zz, src=None):
        where = f2.at[span(t, zz), :]
        i = t * rows_n + zz
        send(where if src is None else src, where, cs_sem.at[i], ag_recv.at[i], sib)

    def to_y(k, zz, src=None):
        where = f2.at[span(blk, zz), :]
        send(where if src is None else src, where, ys_sem.at[k - 1, zz],
             ag_recv.at[blk * rows_n + zz], {"blk": at_y(k) * CORES + core})

    order = sorted(range(1, rows_n), key=lambda k: -min(k, rows_n - k))
    own = f2.at[span(blk, z), :]
    for k in order:
        send(f2_in, own, zs_sem.at[k - 1], ag_recv.at[blk * rows_n + z], {"rows": at_z(k)})
    for k in range(1, ys_n):
        to_y(k, z, f2_in)
    to_sib(blk, z, f2_in)

    loads["f1"].wait()
    high, low = split(f1[...])
    f1s[0:band, :] = high
    f1s[band:, :] = low
    turned = f1[...].T
    high, low = split(turned)
    f1t[:, 0:band] = high
    f1t[:, band:] = low
    loads["c3"].wait()
    loads["c2"].wait()
    loads["c1"].wait()
    c3 = c3t[...].T
    for t in range(tiles):
        coarse[t] = jnp.concatenate(
            [c1[:, t * POOL1:(t + 1) * POOL1], c2[:, t * POOL2:(t + 1) * POOL2],
             c3[:, t * POOL3:(t + 1) * POOL3],
             jnp.zeros((band, POOLED - POOL1 - POOL2 - POOL3), f32)], axis=1)
    loads["c0"].wait()

    def band_sum(t):
        high, low = split(coarse[t])
        spread = mm(jnp.concatenate([high, low], axis=0), table[...], 1, 1)
        total = c0[:, pl.ds(pl.multiple_of(t * TILE, TILE), TILE)] + (spread[:band] + spread[band:])
        high, low = split(total * inv_root)
        scaled[t, 0:band, :] = high
        scaled[t, band:, :] = low
        twice = jnp.concatenate([high, high], axis=0)
        value = mm(f1t[...], twice, 1, 0) + mm(f1t[:, 0:band], low, 1, 0)
        acc[t] = value.reshape(rows_n, chans // rows_n, TILE)

    for k in list(range(1, ys_n)) + [0]:
        yy = at_y(k)
        band_sum(yy * CORES + other)
        send(acc.at[yy * CORES + other], cin.at[yy], rc_send.at[yy], rc_recv.at[yy], sib)
        band_sum(yy * CORES + core)

    def chip_sum(yy):
        await_(cin.at[yy], rc_recv.at[yy])
        t = yy * CORES + core
        acc[t] += cin[yy]

    for k in range(1, ys_n):
        yy = at_y(k)
        chip_sum(yy)
        for j in order + [0]:
            zz = at_z(j)
            send(acc.at[yy * CORES + core, zz], yin.at[k - 1, zz], ry_send.at[k - 1, zz],
                 ry_recv.at[k - 1, zz], {"blk": yy * CORES + core})

    for k in reversed(order):
        zz = at_z(k)
        ag_wait(blk, zz)
        for j in range(1, ys_n):
            to_y(j, zz)
        to_sib(blk, zz)
    chip_sum(y)
    loads["f2"].wait()

    def tile_work(i, t):
        block = f2[pl.ds(pl.multiple_of(t * TILE, TILE), TILE), :]
        high, low = split(block)
        both = mm(f1s[...], high, 1, 1)
        value = (both[:band] + both[band:] + mm(f1s[0:band, :], low, 1, 1)) * inv_root
        o0[:, pl.ds(pl.multiple_of(t * TILE, TILE), TILE)] = value
        vh, vl = split(value)
        both = mm(jnp.concatenate([vh, vl], axis=0), table[...], 1, 0)
        both = both[:band] + both[band:]
        pooled[t] = both[:, POOL1:]
        o1[:, pl.ds(pl.multiple_of(t * POOL1, POOL1), POOL1)] = both[:, :POOL1]
        both = mm(scaled[t], high, 1, 0)
        grad = both[:band] + both[band:] + mm(scaled[t, 0:band, :], low, 1, 0)
        if i == 0:
            gacc[...] = grad
        else:
            gacc[...] += grad

    tile_work(0, blk)

    for j in order + [0]:
        zz = at_z(j)
        for k in range(1, ys_n):
            await_(yin.at[k - 1, zz], ry_recv.at[k - 1, zz])
            acc[blk, zz] += yin[k - 1, zz]
        if j:
            send(acc.at[blk, zz], zin.at[j - 1], rz_send.at[j - 1], rz_recv.at[j - 1], {"rows": zz})

    for zz in range(rows_n):
        ag_wait(y * CORES + other, zz)
    tile_work(1, y * CORES + other)

    done = 2
    for k in range(1, ys_n):
        t = at_y(k) * CORES + core
        for j in [0] + list(reversed(order)):
            zz = at_z(j)
            ag_wait(t, zz)
            to_sib(t, zz)
        tile_work(done, t)
        done += 1
    for k in range(1, ys_n):
        t = at_y(k) * CORES + other
        for zz in range(rows_n):
            ag_wait(t, zz)
        tile_work(done, t)
        done += 1

    g1t[...] = gacc[...].T.reshape(rows_n, chans // rows_n, band)
    mine = pl.ds(pl.multiple_of(z * band, band), band)
    for k in order:
        zz = at_z(k)
        send(g1t.at[zz], g1_out.at[:, mine], g_send.at[k - 1], g_recv.at[k - 1], {"rows": zz})
    g1_out[:, mine] = g1t[z]
    o2[...] = jnp.concatenate([pooled[t, :, :POOL2] for t in range(tiles)], axis=1)
    o3[...] = jnp.concatenate([pooled[t, :, POOL2:POOL2 + POOL3] for t in range(tiles)], axis=1).T
    total = acc[blk, z]
    for k in range(1, rows_n):
        await_(zin.at[k - 1], rz_recv.at[k - 1])
        total += zin[k - 1]
    g2_out[...] = total
    for k in range(1, rows_n):
        zz = (z + rows_n - k) % rows_n
        await_(g1_out.at[:, pl.ds(pl.multiple_of(zz * band, band), band)], g_recv.at[k - 1])
    for copy in sent:
        copy.wait_send()


def store(*refs):
    sems = refs[12]
    copies = [pltpu.make_async_copy(refs[i], refs[6 + i], sems.at[i]) for i in range(6)]
    for copy in copies:
        copy.start()
    for copy in copies:
        copy.wait()


def on_device(tiles, rows_n, frame_one, frame_two, cot_zero, cot_one, cot_two, cot_three):
    band, chans = frame_one.shape
    ys_n = tiles // CORES
    part = chans // rows_n
    cots = (cot_zero, cot_one, cot_two, cot_three)
    hbm = pl.BlockSpec(memory_space=pl.ANY)
    vmem = pl.BlockSpec(memory_space=pltpu.VMEM)
    dma = pltpu.SemaphoreType.DMA
    shapes = tuple(cot.shape for cot in cots[:3]) + (
        cot_three.shape[::-1], (part, band * rows_n), (part, TILE))
    made = pl.pallas_call(
        functools.partial(kernel, tiles, rows_n),
        out_shape=tuple(pltpu.VMEM(shape, f32) for shape in shapes),
        in_specs=[pl.BlockSpec(memory_space=pltpu.HBM)] * 6,
        out_specs=(vmem,) * 6,
        scratch_shapes=[
            pltpu.VMEM((band, chans), f32),
            pltpu.VMEM((tiles * TILE, chans), f32),
            pltpu.VMEM(cot_zero.shape, f32),
            pltpu.VMEM(cot_one.shape, f32),
            pltpu.VMEM(cot_two.shape, f32),
            pltpu.VMEM(cot_three.shape[::-1], f32),
            pltpu.VMEM((tiles, band, POOLED), f32),
            pltpu.VMEM((tiles, 2 * band, TILE), bf16),
            pltpu.VMEM((TILE, POOLED), bf16),
            pltpu.VMEM((2 * band, chans), bf16),
            pltpu.VMEM((chans, 2 * band), bf16),
            pltpu.VMEM((tiles, rows_n, part, TILE), f32),
            pltpu.VMEM((ys_n, rows_n, part, TILE), f32),
            pltpu.VMEM((ys_n - 1, rows_n, part, TILE), f32),
            pltpu.VMEM((rows_n - 1, part, TILE), f32),
            pltpu.VMEM((tiles, band, POOLED - POOL1), f32),
            pltpu.VMEM((band, chans), f32),
            pltpu.VMEM((rows_n, part, band), f32),
            dma((6,)),
            dma((tiles * rows_n,)),
            dma((rows_n - 1,)),
            dma((ys_n - 1, rows_n)),
            dma((tiles * rows_n,)),
            dma((ys_n,)), dma((ys_n,)),
            dma((ys_n - 1, rows_n)), dma((ys_n - 1, rows_n)),
            dma((rows_n - 1,)), dma((rows_n - 1,)),
            dma((rows_n - 1,)), dma((rows_n - 1,)),
        ],
        compiler_params=pltpu.CompilerParams(
            collective_id=0, has_side_effects=True, vmem_limit_bytes=48 << 20),
    )(*[pltpu.with_memory_space_constraint(value, pltpu.HBM) for value in (
        frame_one, frame_two, cot_zero, cot_one, cot_two, cot_three.T)])
    placed = pl.pallas_call(
        store,
        out_shape=tuple(jax.ShapeDtypeStruct(shape, f32) for shape in shapes),
        in_specs=[hbm] * 6,
        out_specs=(hbm,) * 6,
        scratch_shapes=[dma((6,))],
        compiler_params=pltpu.CompilerParams(vmem_limit_bytes=1 << 20),
    )(*[pltpu.with_memory_space_constraint(value, pltpu.VMEM) for value in made])
    return placed[:3] + (placed[3].T,) + placed[4:]


def solution(mesh):
    band = P(("groups", "blk", "rows"), None)
    turned = P("rows", ("groups", "blk"))
    return jax.shard_map(
        functools.partial(on_device, mesh.shape["blk"], mesh.shape["rows"]),
        mesh=mesh,
        in_specs=(band,) * 6,
        out_specs=(band,) * 4 + (turned,) * 2,
        check_vma=False,
    )
```

```python
import functools
import math

import jax
import jax.numpy as jnp
from jax import lax
from jax.experimental import pallas as pl
from jax.experimental.pallas import tpu as pltpu
from jax.sharding import PartitionSpec as P

TROWS = 8
W2 = 64
CORES = 2
TILE = TROWS * W2
POOL1 = TILE // 4
POOL2 = TILE // 16
POOL3 = TILE // 64
POOLED = 2 * POOL1

f32 = jnp.float32
bf16 = jnp.bfloat16


def split(x):
    high = x.astype(bf16)
    low = (x - high.astype(f32)).astype(bf16)
    return high, low


def mm(a, b, ca, cb):
    return lax.dot_general(a, b, (((ca,), (cb,)), ((), ())), preferred_element_type=f32)


def pool_table():
    shape = (TILE, POOLED)
    pixel = lax.broadcasted_iota(jnp.int32, (TILE, 1), 0)
    row, col = pixel // W2, pixel % W2
    one = lax.shift_right_logical(row, 1) * (W2 // 2) + lax.shift_right_logical(col, 1)
    two = lax.shift_right_logical(row, 2) * (W2 // 4) + lax.shift_right_logical(col, 2) + POOL1
    three = lax.shift_right_logical(row, 3) * (W2 // 8) + lax.shift_right_logical(col, 3) + (
        POOL1 + POOL2)
    slot = lax.broadcasted_iota(jnp.int32, shape, 1)
    value = jnp.where(slot == one, 0.25, 0.0)
    value = jnp.where(slot == two, 0.0625, value)
    value = jnp.where(slot == three, 0.015625, value)
    return value.astype(bf16)


def kernel(tiles, rows_n, f1_in, f2_in, c0_in, c1_in, c2_in, c3_in,
           o0, o1, o2, o3, g1_out, g2_out,
           f1, f2, c0, c1, c2, c3t, coarse, scaled, table, f1s, f1t, acc, cin, yin, zin,
           pooled, gacc, g1t,
           in_sem, ag_recv, zs_sem, ys_sem, cs_sem,
           rc_send, rc_recv, ry_send, ry_recv, rz_send, rz_recv, g_send, g_recv):
    band = f1.shape[0]
    chans = f1.shape[1]
    band2 = f2_in.shape[0]
    ys_n = tiles // CORES
    inv_root = 1.0 / math.sqrt(chans)
    blk = lax.axis_index("blk")
    z = lax.axis_index("rows")
    core = blk % CORES
    y = blk // CORES
    other = 1 - core
    sib = {"blk": y * CORES + other}

    def at_z(k):
        return (z + k) % rows_n

    def at_y(k):
        return (y + k) % ys_n

    def span(t, zz):
        return pl.ds(pl.multiple_of(t * TILE + zz * band2, 8), band2)

    loads = {}
    for i, (name, src, dst) in enumerate((
            ("f1", f1_in, f1), ("c3", c3_in, c3t), ("c2", c2_in, c2), ("c1", c1_in, c1),
            ("c0", c0_in, c0), ("f2", f2_in, f2.at[span(blk, z), :]))):
        loads[name] = pltpu.make_async_copy(src, dst, in_sem.at[i])
        loads[name].start()

    peers = [{"rows": at_z(k)} for k in range(1, rows_n)]
    peers += [{"blk": at_y(k) * CORES + core} for k in range(1, ys_n)]
    peers += [sib]
    barrier = pltpu.get_barrier_semaphore()
    for peer in peers:
        pl.semaphore_signal(barrier, inc=1, device_id=peer)
    pl.semaphore_wait(barrier, len(peers))

    sent = []

    def send(src, dst, ssem, rsem, peer):
        copy = pltpu.make_async_remote_copy(
            src_ref=src, dst_ref=dst, send_sem=ssem, recv_sem=rsem,
            device_id=peer, device_id_type=pl.DeviceIdType.MESH)
        copy.start()
        sent.append(copy)

    def await_(ref, rsem):
        pltpu.make_async_copy(ref, ref, rsem).wait()

    def ag_wait(t, zz):
        await_(f2.at[span(t, zz), :], ag_recv.at[t * rows_n + zz])

    def to_sib(t, zz, src=None):
        where = f2.at[span(t, zz), :]
        i = t * rows_n + zz
        send(where if src is None else src, where, cs_sem.at[i], ag_recv.at[i], sib)

    def to_y(k, zz, src=None):
        where = f2.at[span(blk, zz), :]
        send(where if src is None else src, where, ys_sem.at[k - 1, zz],
             ag_recv.at[blk * rows_n + zz], {"blk": at_y(k) * CORES + core})

    order = sorted(range(1, rows_n), key=lambda k: -min(k, rows_n - k))
    own = f2.at[span(blk, z), :]
    for k in order:
        send(f2_in, own, zs_sem.at[k - 1], ag_recv.at[blk * rows_n + z], {"rows": at_z(k)})
    for k in range(1, ys_n):
        to_y(k, z, f2_in)
    to_sib(blk, z, f2_in)

    table[...] = pool_table()
    loads["f1"].wait()
    high, low = split(f1[...])
    f1s[0:band, :] = high
    f1s[band:, :] = low
    turned = f1[...].T
    high, low = split(turned)
    f1t[:, 0:band] = high
    f1t[:, band:] = low
    loads["c3"].wait()
    loads["c2"].wait()
    loads["c1"].wait()
    c3 = c3t[...].T
    for t in range(tiles):
        coarse[t] = jnp.concatenate(
            [c1[:, t * POOL1:(t + 1) * POOL1], c2[:, t * POOL2:(t + 1) * POOL2],
             c3[:, t * POOL3:(t + 1) * POOL3],
             jnp.zeros((band, POOLED - POOL1 - POOL2 - POOL3), f32)], axis=1)
    loads["c0"].wait()

    def band_sum(t):
        high, low = split(coarse[t])
        spread = mm(jnp.concatenate([high, low], axis=0), table[...], 1, 1)
        total = c0[:, pl.ds(pl.multiple_of(t * TILE, TILE), TILE)] + (spread[:band] + spread[band:])
        high, low = split(total * inv_root)
        scaled[t, 0:band, :] = high
        scaled[t, band:, :] = low
        twice = jnp.concatenate([high, high], axis=0)
        value = mm(f1t[...], twice, 1, 0) + mm(f1t[:, 0:band], low, 1, 0)
        acc[t] = value.reshape(rows_n, chans // rows_n, TILE)

    for k in list(range(1, ys_n)) + [0]:
        yy = at_y(k)
        band_sum(yy * CORES + other)
        send(acc.at[yy * CORES + other], cin.at[yy], rc_send.at[yy], rc_recv.at[yy], sib)
        band_sum(yy * CORES + core)

    def chip_sum(yy):
        await_(cin.at[yy], rc_recv.at[yy])
        t = yy * CORES + core
        acc[t] += cin[yy]

    pieces = order + [0]
    early, late = pieces[:rows_n - 1], pieces[rows_n - 1:]

    def sums_to_y(k, some):
        yy = at_y(k)
        for j in some:
            zz = at_z(j)
            send(acc.at[yy * CORES + core, zz], yin.at[k - 1, zz], ry_send.at[k - 1, zz],
                 ry_recv.at[k - 1, zz], {"blk": yy * CORES + core})

    for k in range(1, ys_n):
        chip_sum(at_y(k))
        sums_to_y(k, early)

    for k in reversed(order):
        zz = at_z(k)
        ag_wait(blk, zz)
        for j in range(1, ys_n):
            to_y(j, zz)
        to_sib(blk, zz)
    for k in range(1, ys_n):
        sums_to_y(k, late)
    chip_sum(y)
    loads["f2"].wait()

    def tile_work(i, t):
        block = f2[pl.ds(pl.multiple_of(t * TILE, TILE), TILE), :]
        high, low = split(block)
        both = mm(f1s[...], high, 1, 1)
        value = (both[:band] + both[band:] + mm(f1s[0:band, :], low, 1, 1)) * inv_root
        o0[:, pl.ds(pl.multiple_of(t * TILE, TILE), TILE)] = value
        vh, vl = split(value)
        both = mm(jnp.concatenate([vh, vl], axis=0), table[...], 1, 0)
        both = both[:band] + both[band:]
        pooled[t] = both[:, POOL1:]
        o1[:, pl.ds(pl.multiple_of(t * POOL1, POOL1), POOL1)] = both[:, :POOL1]
        both = mm(scaled[t], high, 1, 0)
        grad = both[:band] + both[band:] + mm(scaled[t, 0:band, :], low, 1, 0)
        if i == 0:
            gacc[...] = grad
        else:
            gacc[...] += grad

    tile_work(0, blk)

    def sums_to_rows(some):
        for j in some:
            zz = at_z(j)
            for k in range(1, ys_n):
                await_(yin.at[k - 1, zz], ry_recv.at[k - 1, zz])
                acc[blk, zz] += yin[k - 1, zz]
            if j:
                send(acc.at[blk, zz], zin.at[j - 1], rz_send.at[j - 1], rz_recv.at[j - 1],
                     {"rows": zz})

    sums_to_rows(early)

    for zz in range(rows_n):
        ag_wait(y * CORES + other, zz)
    tile_work(1, y * CORES + other)

    done = 2
    for k in range(1, ys_n):
        t = at_y(k) * CORES + core
        for j in [0] + list(reversed(order)):
            zz = at_z(j)
            ag_wait(t, zz)
            to_sib(t, zz)
        tile_work(done, t)
        done += 1
    for k in range(1, ys_n):
        t = at_y(k) * CORES + other
        for zz in range(rows_n):
            ag_wait(t, zz)
        tile_work(done, t)
        done += 1

    g1t[...] = gacc[...].T.reshape(rows_n, chans // rows_n, band)
    mine = pl.ds(pl.multiple_of(z * band, band), band)
    for k in order:
        zz = at_z(k)
        send(g1t.at[zz], g1_out.at[:, mine], g_send.at[k - 1], g_recv.at[k - 1], {"rows": zz})
    g1_out[:, mine] = g1t[z]
    sums_to_rows(late)
    o2[...] = jnp.concatenate([pooled[t, :, :POOL2] for t in range(tiles)], axis=1)
    o3[...] = jnp.concatenate([pooled[t, :, POOL2:POOL2 + POOL3] for t in range(tiles)], axis=1).T
    total = acc[blk, z]
    for k in range(1, rows_n):
        await_(zin.at[k - 1], rz_recv.at[k - 1])
        total += zin[k - 1]
    g2_out[...] = total
    for k in range(1, rows_n):
        zz = (z + rows_n - k) % rows_n
        await_(g1_out.at[:, pl.ds(pl.multiple_of(zz * band, band), band)], g_recv.at[k - 1])
    for copy in sent:
        copy.wait_send()


def store(*refs):
    sems = refs[12]
    copies = [pltpu.make_async_copy(refs[i], refs[6 + i], sems.at[i]) for i in range(6)]
    for copy in copies:
        copy.start()
    for copy in copies:
        copy.wait()


def on_device(tiles, rows_n, frame_one, frame_two, cot_zero, cot_one, cot_two, cot_three):
    band, chans = frame_one.shape
    ys_n = tiles // CORES
    part = chans // rows_n
    cots = (cot_zero, cot_one, cot_two, cot_three)
    hbm = pl.BlockSpec(memory_space=pl.ANY)
    vmem = pl.BlockSpec(memory_space=pltpu.VMEM)
    dma = pltpu.SemaphoreType.DMA
    shapes = tuple(cot.shape for cot in cots[:3]) + (
        cot_three.shape[::-1], (part, band * rows_n), (part, TILE))
    made = pl.pallas_call(
        functools.partial(kernel, tiles, rows_n),
        out_shape=tuple(pltpu.VMEM(shape, f32) for shape in shapes),
        in_specs=[pl.BlockSpec(memory_space=pltpu.HBM)] * 6,
        out_specs=(vmem,) * 6,
        scratch_shapes=[
            pltpu.VMEM((band, chans), f32),
            pltpu.VMEM((tiles * TILE, chans), f32),
            pltpu.VMEM(cot_zero.shape, f32),
            pltpu.VMEM(cot_one.shape, f32),
            pltpu.VMEM(cot_two.shape, f32),
            pltpu.VMEM(cot_three.shape[::-1], f32),
            pltpu.VMEM((tiles, band, POOLED), f32),
            pltpu.VMEM((tiles, 2 * band, TILE), bf16),
            pltpu.VMEM((TILE, POOLED), bf16),
            pltpu.VMEM((2 * band, chans), bf16),
            pltpu.VMEM((chans, 2 * band), bf16),
            pltpu.VMEM((tiles, rows_n, part, TILE), f32),
            pltpu.VMEM((ys_n, rows_n, part, TILE), f32),
            pltpu.VMEM((ys_n - 1, rows_n, part, TILE), f32),
            pltpu.VMEM((rows_n - 1, part, TILE), f32),
            pltpu.VMEM((tiles, band, POOLED - POOL1), f32),
            pltpu.VMEM((band, chans), f32),
            pltpu.VMEM((rows_n, part, band), f32),
            dma((6,)),
            dma((tiles * rows_n,)),
            dma((rows_n - 1,)),
            dma((ys_n - 1, rows_n)),
            dma((tiles * rows_n,)),
            dma((ys_n,)), dma((ys_n,)),
            dma((ys_n - 1, rows_n)), dma((ys_n - 1, rows_n)),
            dma((rows_n - 1,)), dma((rows_n - 1,)),
            dma((rows_n - 1,)), dma((rows_n - 1,)),
        ],
        compiler_params=pltpu.CompilerParams(
            collective_id=0, has_side_effects=True, vmem_limit_bytes=48 << 20),
    )(*[pltpu.with_memory_space_constraint(value, pltpu.HBM) for value in (
        frame_one, frame_two, cot_zero, cot_one, cot_two, cot_three.T)])
    placed = pl.pallas_call(
        store,
        out_shape=tuple(jax.ShapeDtypeStruct(shape, f32) for shape in shapes),
        in_specs=[hbm] * 6,
        out_specs=(hbm,) * 6,
        scratch_shapes=[dma((6,))],
        compiler_params=pltpu.CompilerParams(vmem_limit_bytes=1 << 20),
    )(*[pltpu.with_memory_space_constraint(value, pltpu.VMEM) for value in made])
    return placed[:3] + (placed[3].T,) + placed[4:]


def solution(mesh):
    band = P(("groups", "blk", "rows"), None)
    turned = P("rows", ("groups", "blk"))
    return jax.shard_map(
        functools.partial(on_device, mesh.shape["blk"], mesh.shape["rows"]),
        mesh=mesh,
        in_specs=(band,) * 6,
        out_specs=(band,) * 4 + (turned,) * 2,
        check_vma=False,
    )
```

```python
import functools
import math

import jax
import jax.numpy as jnp
from jax import lax
from jax.experimental import pallas as pl
from jax.experimental.pallas import tpu as pltpu
from jax.sharding import PartitionSpec as P

TROWS = 8
W2 = 64
CORES = 2
TILE = TROWS * W2
POOL1 = TILE // 4
POOL2 = TILE // 16
POOL3 = TILE // 64
POOLED = 2 * POOL1

f32 = jnp.float32
bf16 = jnp.bfloat16


def split(x):
    high = x.astype(bf16)
    low = (x - high.astype(f32)).astype(bf16)
    return high, low


def mm(a, b, ca, cb):
    return lax.dot_general(a, b, (((ca,), (cb,)), ((), ())), preferred_element_type=f32)


def pool_table():
    shape = (TILE, POOLED)
    pixel = lax.broadcasted_iota(jnp.int32, (TILE, 1), 0)
    row, col = pixel // W2, pixel % W2
    one = lax.shift_right_logical(row, 1) * (W2 // 2) + lax.shift_right_logical(col, 1)
    two = lax.shift_right_logical(row, 2) * (W2 // 4) + lax.shift_right_logical(col, 2) + POOL1
    three = lax.shift_right_logical(row, 3) * (W2 // 8) + lax.shift_right_logical(col, 3) + (
        POOL1 + POOL2)
    slot = lax.broadcasted_iota(jnp.int32, shape, 1)
    value = jnp.where(slot == one, 0.25, 0.0)
    value = jnp.where(slot == two, 0.0625, value)
    value = jnp.where(slot == three, 0.015625, value)
    return value.astype(bf16)


def kernel(tiles, rows_n, f1_in, f2_in, c0_in, c1_in, c2_in, c3_in,
           o0, o1, o2, o3, g1_out, g2_out,
           f1, f2, c0, c1, c2, c3t, coarse, scaled, table, f1s, f1t, acc, cin, yin, zin,
           pooled, gacc, g1t,
           in_sem, ag_recv, zs_sem, ys_sem, cs_sem,
           rc_send, rc_recv, ry_send, ry_recv, rz_send, rz_recv, g_send, g_recv, zf_sem):
    band = f1.shape[0]
    chans = f1.shape[1]
    band2 = f2_in.shape[0]
    ys_n = tiles // CORES
    inv_root = 1.0 / math.sqrt(chans)
    blk = lax.axis_index("blk")
    z = lax.axis_index("rows")
    core = blk % CORES
    y = blk // CORES
    other = 1 - core
    sib = {"blk": y * CORES + other}

    def at_z(k):
        zz, bit = z, 1
        while bit < rows_n:
            if k % (2 * bit) >= bit:
                zz = zz + bit - 2 * bit * (z // bit % 2)
            bit *= 2
        return zz

    def at_y(k):
        return (y + k) % ys_n

    def span(t, zz):
        return pl.ds(pl.multiple_of(t * TILE + zz * band2, 8), band2)

    loads = {}
    for i, (name, src, dst) in enumerate((
            ("f1", f1_in, f1), ("c3", c3_in, c3t), ("c2", c2_in, c2), ("c1", c1_in, c1),
            ("c0", c0_in, c0), ("f2", f2_in, f2.at[span(blk, z), :]))):
        loads[name] = pltpu.make_async_copy(src, dst, in_sem.at[i])
        loads[name].start()

    peers = [{"rows": at_z(k)} for k in range(1, rows_n)]
    peers += [{"blk": at_y(k) * CORES + core} for k in range(1, ys_n)]
    peers += [sib]
    barrier = pltpu.get_barrier_semaphore()
    for peer in peers:
        pl.semaphore_signal(barrier, inc=1, device_id=peer)
    table[...] = pool_table()
    loads["f1"].wait()
    high, low = split(f1[...])
    f1s[0:band, :] = high
    f1s[band:, :] = low
    turned = f1[...].T
    high, low = split(turned)
    f1t[:, 0:band] = high
    f1t[:, band:] = low
    loads["c3"].wait()
    loads["c2"].wait()
    loads["c1"].wait()
    c3 = c3t[...].T
    for t in range(tiles):
        coarse[t] = jnp.concatenate(
            [c1[:, t * POOL1:(t + 1) * POOL1], c2[:, t * POOL2:(t + 1) * POOL2],
             c3[:, t * POOL3:(t + 1) * POOL3],
             jnp.zeros((band, POOLED - POOL1 - POOL2 - POOL3), f32)], axis=1)
    pl.semaphore_wait(barrier, len(peers))

    sent = []

    def send(src, dst, ssem, rsem, peer):
        copy = pltpu.make_async_remote_copy(
            src_ref=src, dst_ref=dst, send_sem=ssem, recv_sem=rsem,
            device_id=peer, device_id_type=pl.DeviceIdType.MESH)
        copy.start()
        sent.append(copy)

    def await_(ref, rsem):
        pltpu.make_async_copy(ref, ref, rsem).wait()

    def ag_wait(t, zz):
        await_(f2.at[span(t, zz), :], ag_recv.at[t * rows_n + zz])

    def to_sib(t, zz, src=None):
        where = f2.at[span(t, zz), :]
        i = t * rows_n + zz
        send(where if src is None else src, where, cs_sem.at[i], ag_recv.at[i], sib)

    def to_y(k, zz, src=None):
        where = f2.at[span(blk, zz), :]
        send(where if src is None else src, where, ys_sem.at[k - 1, zz],
             ag_recv.at[blk * rows_n + zz], {"blk": at_y(k) * CORES + core})

    order = sorted(range(1, rows_n), key=lambda k: (k & -k, k), reverse=True)
    own = f2.at[span(blk, z), :]
    for k in reversed(order):
        send(f2_in, own, zs_sem.at[k - 1], ag_recv.at[blk * rows_n + z], {"rows": at_z(k)})
    for k in range(1, ys_n):
        to_y(k, z, f2_in)
    to_sib(blk, z, f2_in)

    loads["c0"].wait()

    def band_sum(t):
        high, low = split(coarse[t])
        spread = mm(jnp.concatenate([high, low], axis=0), table[...], 1, 1)
        total = c0[:, pl.ds(pl.multiple_of(t * TILE, TILE), TILE)] + (spread[:band] + spread[band:])
        high, low = split(total * inv_root)
        scaled[t, 0:band, :] = high
        scaled[t, band:, :] = low
        twice = jnp.concatenate([high, high], axis=0)
        value = mm(f1t[...], twice, 1, 0) + mm(f1t[:, 0:band], low, 1, 0)
        acc[t] = value.reshape(rows_n, chans // rows_n, TILE)

    for k in list(range(1, ys_n)) + [0]:
        yy = at_y(k)
        band_sum(yy * CORES + other)
        send(acc.at[yy * CORES + other], cin.at[yy], rc_send.at[yy], rc_recv.at[yy], sib)
        band_sum(yy * CORES + core)

    def chip_sum(yy):
        await_(cin.at[yy], rc_recv.at[yy])
        t = yy * CORES + core
        acc[t] += cin[yy]

    pieces = order + [0]
    early, late = pieces[:rows_n - 1], pieces[rows_n - 1:]

    def sums_to_y(k, some):
        yy = at_y(k)
        for j in some:
            zz = at_z(j)
            send(acc.at[yy * CORES + core, zz], yin.at[k - 1, zz], ry_send.at[k - 1, zz],
                 ry_recv.at[k - 1, zz], {"blk": yy * CORES + core})

    for k in range(1, ys_n):
        chip_sum(at_y(k))
        sums_to_y(k, early)

    for k in range(1, ys_n):
        t = at_y(k) * CORES + core
        ag_wait(t, z)
        where = f2.at[span(t, z), :]
        send(where, where, zf_sem.at[k - 1], ag_recv.at[t * rows_n + z], {"rows": at_z(1)})
        to_sib(t, z)

    for k in reversed(order):
        zz = at_z(k)
        ag_wait(blk, zz)
        if k != 1:
            for j in range(1, ys_n):
                to_y(j, zz)
        to_sib(blk, zz)
    for k in range(1, ys_n):
        sums_to_y(k, late)
    chip_sum(y)
    loads["f2"].wait()

    def tile_work(i, t):
        block = f2[pl.ds(pl.multiple_of(t * TILE, TILE), TILE), :]
        high, low = split(block)
        both = mm(f1s[...], high, 1, 1)
        value = (both[:band] + both[band:] + mm(f1s[0:band, :], low, 1, 1)) * inv_root
        o0[:, pl.ds(pl.multiple_of(t * TILE, TILE), TILE)] = value
        vh, vl = split(value)
        both = mm(jnp.concatenate([vh, vl], axis=0), table[...], 1, 0)
        both = both[:band] + both[band:]
        pooled[t] = both[:, POOL1:]
        o1[:, pl.ds(pl.multiple_of(t * POOL1, POOL1), POOL1)] = both[:, :POOL1]
        both = mm(scaled[t], high, 1, 0)
        grad = both[:band] + both[band:] + mm(scaled[t, 0:band, :], low, 1, 0)
        if i == 0:
            gacc[...] = grad
        else:
            gacc[...] += grad


    def sums_to_rows(some):
        for j in some:
            zz = at_z(j)
            for k in range(1, ys_n):
                await_(yin.at[k - 1, zz], ry_recv.at[k - 1, zz])
                acc[blk, zz] += yin[k - 1, zz]
            if j:
                send(acc.at[blk, zz], zin.at[j - 1], rz_send.at[j - 1], rz_recv.at[j - 1],
                     {"rows": zz})

    sums_to_rows(early)
    tile_work(0, blk)

    for zz in range(rows_n):
        ag_wait(y * CORES + other, zz)
    tile_work(1, y * CORES + other)

    done = 2
    for k in range(1, ys_n):
        t = at_y(k) * CORES + core
        for j in [1] + [k for k in reversed(order) if k != 1]:
            zz = at_z(j)
            ag_wait(t, zz)
            to_sib(t, zz)
        tile_work(done, t)
        done += 1
    for k in range(1, ys_n):
        t = at_y(k) * CORES + other
        for zz in range(rows_n):
            ag_wait(t, zz)
        tile_work(done, t)
        done += 1

    g1t[...] = gacc[...].T.reshape(rows_n, chans // rows_n, band)
    mine = pl.ds(pl.multiple_of(z * band, band), band)
    for k in order:
        zz = at_z(k)
        send(g1t.at[zz], g1_out.at[:, mine], g_send.at[k - 1], g_recv.at[k - 1], {"rows": zz})
    g1_out[:, mine] = g1t[z]
    sums_to_rows(late)
    o2[...] = jnp.concatenate([pooled[t, :, :POOL2] for t in range(tiles)], axis=1)
    o3[...] = jnp.concatenate([pooled[t, :, POOL2:POOL2 + POOL3] for t in range(tiles)], axis=1).T
    total = acc[blk, z]
    for k in range(1, rows_n):
        await_(zin.at[k - 1], rz_recv.at[k - 1])
        total += zin[k - 1]
    g2_out[...] = total
    for k in range(1, rows_n):
        zz = at_z(k)
        await_(g1_out.at[:, pl.ds(pl.multiple_of(zz * band, band), band)], g_recv.at[k - 1])
    for copy in sent:
        copy.wait_send()


def store(*refs):
    sems = refs[12]
    copies = [pltpu.make_async_copy(refs[i], refs[6 + i], sems.at[i]) for i in range(6)]
    for copy in copies:
        copy.start()
    for copy in copies:
        copy.wait()


def on_device(tiles, rows_n, frame_one, frame_two, cot_zero, cot_one, cot_two, cot_three):
    band, chans = frame_one.shape
    ys_n = tiles // CORES
    part = chans // rows_n
    cots = (cot_zero, cot_one, cot_two, cot_three)
    hbm = pl.BlockSpec(memory_space=pl.ANY)
    vmem = pl.BlockSpec(memory_space=pltpu.VMEM)
    dma = pltpu.SemaphoreType.DMA
    shapes = tuple(cot.shape for cot in cots[:3]) + (
        cot_three.shape[::-1], (part, band * rows_n), (part, TILE))
    made = pl.pallas_call(
        functools.partial(kernel, tiles, rows_n),
        out_shape=tuple(pltpu.VMEM(shape, f32) for shape in shapes),
        in_specs=[pl.BlockSpec(memory_space=pltpu.HBM)] * 6,
        out_specs=(vmem,) * 6,
        scratch_shapes=[
            pltpu.VMEM((band, chans), f32),
            pltpu.VMEM((tiles * TILE, chans), f32),
            pltpu.VMEM(cot_zero.shape, f32),
            pltpu.VMEM(cot_one.shape, f32),
            pltpu.VMEM(cot_two.shape, f32),
            pltpu.VMEM(cot_three.shape[::-1], f32),
            pltpu.VMEM((tiles, band, POOLED), f32),
            pltpu.VMEM((tiles, 2 * band, TILE), bf16),
            pltpu.VMEM((TILE, POOLED), bf16),
            pltpu.VMEM((2 * band, chans), bf16),
            pltpu.VMEM((chans, 2 * band), bf16),
            pltpu.VMEM((tiles, rows_n, part, TILE), f32),
            pltpu.VMEM((ys_n, rows_n, part, TILE), f32),
            pltpu.VMEM((ys_n - 1, rows_n, part, TILE), f32),
            pltpu.VMEM((rows_n - 1, part, TILE), f32),
            pltpu.VMEM((tiles, band, POOLED - POOL1), f32),
            pltpu.VMEM((band, chans), f32),
            pltpu.VMEM((rows_n, part, band), f32),
            dma((6,)),
            dma((tiles * rows_n,)),
            dma((rows_n - 1,)),
            dma((ys_n - 1, rows_n)),
            dma((tiles * rows_n,)),
            dma((ys_n,)), dma((ys_n,)),
            dma((ys_n - 1, rows_n)), dma((ys_n - 1, rows_n)),
            dma((rows_n - 1,)), dma((rows_n - 1,)),
            dma((rows_n - 1,)), dma((rows_n - 1,)),
            dma((ys_n - 1,)),
        ],
        compiler_params=pltpu.CompilerParams(
            collective_id=0, has_side_effects=True, vmem_limit_bytes=48 << 20),
    )(*[pltpu.with_memory_space_constraint(value, pltpu.HBM) for value in (
        frame_one, frame_two, cot_zero, cot_one, cot_two, cot_three.T)])
    placed = pl.pallas_call(
        store,
        out_shape=tuple(jax.ShapeDtypeStruct(shape, f32) for shape in shapes),
        in_specs=[hbm] * 6,
        out_specs=(hbm,) * 6,
        scratch_shapes=[dma((6,))],
        compiler_params=pltpu.CompilerParams(vmem_limit_bytes=1 << 20),
    )(*[pltpu.with_memory_space_constraint(value, pltpu.VMEM) for value in made])
    return placed[:3] + (placed[3].T,) + placed[4:]


def solution(mesh):
    band = P(("groups", "blk", "rows"), None)
    turned = P("rows", ("groups", "blk"))
    return jax.shard_map(
        functools.partial(on_device, mesh.shape["blk"], mesh.shape["rows"]),
        mesh=mesh,
        in_specs=(band,) * 6,
        out_specs=(band,) * 4 + (turned,) * 2,
        check_vma=False,
    )
```
